512 devices in a mesh: space: 128 (over y, z, x_lo), dp: 4 (over x_hi, core).
Axes of the slice: x: 4 (x_hi: 2, x_lo: 2; x = x_hi * 2 + x_lo), y: 4, z: 16, core: 2. Of those that a mesh axis runs over, the one named last changes fastest.
Arguments:
- features: bfloat16 [4, 4096, 4, 128], P('dp', 'space'), may hold values from -6 to 6
- offsets: float32 [4, 4096, 3, 4], P('dp', 'space'), may hold values from 0 to 1
- counts: int32 [4, 4096], P('dp', 'space'), may hold values from 1 to 4
- in_weight: bfloat16 [128, 128], replicated, may hold values from -0.5 to 0.5
- mid_weight: bfloat16 [128, 128], replicated, may hold values from -0.5 to 0.5
- out_weight: bfloat16 [128, 128], replicated, may hold values from -0.5 to 0.5
- rbf_weight: bfloat16 [25, 128], replicated, may hold values from -4 to 4
- filter_weight: bfloat16 [128, 128], replicated, may hold values from -0.5 to 0.5
- readout: bfloat16 [128], replicated, may hold values from -6 to 6
- target: float32 [4], P('dp'), may hold values from -4 to 4
Outputs:
- updated: bfloat16 [4, 4096, 4, 128], P('dp', 'space')
- grad_in: float32 [128, 128], replicated
- grad_mid: float32 [128, 128], replicated
- grad_out: float32 [128, 128], replicated
- grad_rbf: float32 [25, 128], replicated
- grad_filter: float32 [128, 128], replicated
The draws below stay inside these ranges and needn't reach their ends.
Inputs may be any that keep to these rules, and one draw needn't show every extreme that they name: The number of occupied slots of each cell, slots 0 to counts - 1 being occupied.
All inputs are finite; a program needn't handle non-finite values.
Results may differ from the reference program's by a relative error of at most 0.0069.
Values may be sent and summed in bfloat16 or wider, within the bound.
No kernel may reach another device: no remote copies, remote signals or barrier semaphores. Data moves between devices by JAX's collectives and lax.ppermute only.
A program may use at most 64 MiB of HBM per device.

```python
import math
import jax
import jax.numpy as jnp
from jax import lax

F = 128
K = 25
P_SIZE = 4
BX = 2
BY = 4
BZ = 4
DEV_X = 1
DEV_Y = 2
DEV_Z = 4
CELLS = 32
BRICKS = 128
NCELL = 4096
SNAPS = 4


def touch_ends(values, own_key, low, top_value):
    place = [jax.random.randint(jax.random.fold_in(own_key, axis), (), 0, length) for axis, length in enumerate(values.shape)]
    main_axis = values.shape.index(max(values.shape))
    next_to = place[:main_axis] + [(place[main_axis] + 1) % values.shape[main_axis]] + place[main_axis + 1:]
    return values.at[tuple(place)].set(low).at[tuple(next_to)].set(top_value)


def steps_of(own_key, shape, shards, low, top_value):
    def one(axis_at, blocks):
        steps = jax.random.uniform(jax.random.fold_in(jax.random.fold_in(own_key, 6), axis_at), (blocks,), jnp.float32, low / len(shards), top_value / len(shards))
        return jnp.repeat(jnp.exp(steps), shape[axis_at] // blocks).reshape((-1,) + (1,) * (len(shape) - axis_at - 1))

    level = one(*shards[0])
    for cut in shards[1:]:
        level = level * one(*cut)
    return level


def scatter_about(rng, shape, spread, reach, cuts=(), kind=jnp.bfloat16):
    values = spread * jax.random.normal(rng, shape, jnp.float32)
    if cuts:
        values = values * steps_of(rng, shape, cuts, -0.22, 0.18)
    return jnp.clip(values, -reach, reach).astype(kind)


def setup_inputs(seed: int = 0) -> dict:
    seeds = jax.random.split(jax.random.key(seed), 11)
    return {
        "features": scatter_about(seeds[0], (SNAPS, NCELL, P_SIZE, F), 1.0, 6.0, ((0, 4), (1, 128))),
        "offsets": jnp.clip(1.0 * jax.random.uniform(seeds[1], (SNAPS, NCELL, 3, P_SIZE), jnp.float32) ** steps_of(seeds[1], (SNAPS, NCELL, 3, P_SIZE), ((0, 4), (1, 128)), -0.2, 0.2), 0.0, 1.0),
        "counts": touch_ends(jax.random.randint(seeds[2], (SNAPS, NCELL), 1, P_SIZE + 1), jax.random.fold_in(seeds[2], 1), 1, P_SIZE).astype(jnp.int32),
        "in_weight": scatter_about(seeds[3], (F, F), F ** -0.5, 0.5),
        "mid_weight": scatter_about(seeds[4], (F, F), F ** -0.5, 0.5),
        "out_weight": scatter_about(seeds[5], (F, F), F ** -0.5, 0.5),
        "rbf_weight": scatter_about(seeds[6], (K, F), 0.6, 4.0),
        "filter_weight": scatter_about(seeds[7], (F, F), F ** -0.5, 0.5),
        "readout": scatter_about(seeds[8], (F,), 1.0, 6.0),
        "target": scatter_about(seeds[9], (SNAPS,), 1.0, 4.0, ((0, 4),), jnp.float32),
    }


cutoff = 1.0

def shifted_ssp(values):
    return jax.nn.softplus(values) - math.log(2.0)

def extend_brick(blocks_all, strides):
    for axis_pos, stride in zip((1, 2, 3), strides):
        extent = blocks_all.shape[axis_pos]
        lower = jnp.roll(lax.slice_in_dim(blocks_all, extent - 1, extent, axis=axis_pos), stride, axis=0)
        upper = jnp.roll(lax.slice_in_dim(blocks_all, 0, 1, axis=axis_pos), -stride, axis=0)
        blocks_all = jnp.concatenate([lower, blocks_all, upper], axis=axis_pos)
    return blocks_all

def pair_tile(window_geometry, rbf_weight, filter_weight):
    slot_count = window_geometry.shape[2]
    centre = jnp.arange(27)
    cell_shift = jnp.stack([centre // 9 - 1, centre // 3 % 3 - 1, centre % 3 - 1], axis=1).astype(jnp.float32)
    own_places = window_geometry[13, :3, :]
    neighbour_places = window_geometry[:, :3, :] + cell_shift[:, :, None]
    separation = neighbour_places[None, :, :, :] - jnp.transpose(own_places)[:, None, :, None]
    distance = jnp.sqrt(lax.optimization_barrier(jnp.sum(separation * separation, axis=2)))
    slots_here = jnp.arange(slot_count)
    itself = (centre[None, :, None] == 13) & (slots_here[None, None, :] == slots_here[:, None, None])
    inside = (distance < cutoff) & jnp.logical_not(itself)
    smooth = 0.5 * (jnp.cos(math.pi * distance / cutoff) + 1.0)
    weight = jnp.where(inside, smooth, 0.0) * window_geometry[None, :, 3, :]
    distance = distance.reshape(-1)
    weight = weight.reshape(-1)
    centers = jnp.arange(K).astype(jnp.float32) * (cutoff / (K - 1))
    sharpness = (K - 1) * (K - 1) / 2.0
    gaussians = jnp.exp(-sharpness * (distance[None, :] - centers[:, None]) ** 2).astype(jnp.bfloat16)
    pre_filter = lax.dot_general(gaussians, rbf_weight, (((0,), (0,)), ((), ())), preferred_element_type=jnp.float32)
    squashed = shifted_ssp(pre_filter).astype(jnp.bfloat16)
    filter_base = jnp.dot(squashed, filter_weight, preferred_element_type=jnp.float32)
    filters = (filter_base * weight[:, None]).astype(jnp.bfloat16)
    return (gaussians, pre_filter, squashed, filters, weight)

def cell_window(extended, brick, pos_x, pos_y, pos_z):
    anchor = jnp.zeros((), jnp.int32)
    corner = (brick, pos_x, pos_y, pos_z) + (anchor,) * (extended.ndim - 4)
    shape_out = (1, 3, 3, 3) + extended.shape[4:]
    return lax.dynamic_slice(extended, corner, shape_out).reshape((27,) + extended.shape[4:])

def snapshot(features, offsets, counts, in_weight, mid_weight, out_weight, rbf_weight, filter_weight, readout):
    strides = (DEV_X, DEV_Y, DEV_Z)
    occupied = (jnp.arange(P_SIZE)[None, :] < counts[:, None]).astype(jnp.float32)
    geometry = jnp.concatenate([offsets, occupied[:, None, :]], axis=1)
    geometry_ext = extend_brick(geometry.reshape(BRICKS, BX, BY, BZ, 4, P_SIZE), strides)
    flat_features = features.reshape(NCELL * P_SIZE, F)
    hidden = jnp.dot(flat_features, in_weight, preferred_element_type=jnp.float32).astype(jnp.bfloat16)
    hidden_ext = extend_brick(hidden.reshape(BRICKS, BX, BY, BZ, P_SIZE, F), strides)

    def locate(cell_id):
        brick = cell_id // CELLS
        within = cell_id % CELLS
        return (brick, within // (BY * BZ), within // BZ % BY, within % BZ)

    def forward_cell(cell_id):
        brick, pos_x, pos_y, pos_z = locate(cell_id)
        window_geometry = cell_window(geometry_ext, brick, pos_x, pos_y, pos_z)
        pieces = pair_tile(window_geometry, rbf_weight, filter_weight)
        filters = pieces[3].reshape(P_SIZE, 27 * P_SIZE, F).astype(jnp.float32)
        sources = cell_window(hidden_ext, brick, pos_x, pos_y, pos_z).reshape(27 * P_SIZE, F).astype(jnp.float32)
        return jnp.einsum('jf,ijf->if', sources, filters)
    message = lax.map(forward_cell, jnp.arange(NCELL, dtype=jnp.int32)).reshape(NCELL * P_SIZE, F)
    message_low = message.astype(jnp.bfloat16)
    inner = jnp.dot(message_low, mid_weight, preferred_element_type=jnp.float32)
    activation = shifted_ssp(inner).astype(jnp.bfloat16)
    updated = (flat_features.astype(jnp.float32) + jnp.dot(activation, out_weight, preferred_element_type=jnp.float32)).astype(jnp.bfloat16)
    occupied_flat = occupied.reshape(-1)
    energy = jnp.dot(updated, readout, preferred_element_type=jnp.float32)
    energy_sum = jnp.sum(energy * occupied_flat)
    live_total = jnp.sum(occupied_flat)
    start_grad = (occupied_flat[:, None] * readout[None, :].astype(jnp.float32)).astype(jnp.bfloat16)
    grad_out = jnp.dot(activation.T, start_grad, preferred_element_type=jnp.float32)
    back_inner = (jnp.dot(start_grad, out_weight.T, preferred_element_type=jnp.float32) * jax.nn.sigmoid(inner)).astype(jnp.bfloat16)
    grad_mid = jnp.dot(message_low.T, back_inner, preferred_element_type=jnp.float32)
    cotangent = jnp.dot(back_inner, mid_weight.T, preferred_element_type=jnp.float32).astype(jnp.bfloat16)
    cotangent_ext = extend_brick(cotangent.reshape(BRICKS, BX, BY, BZ, P_SIZE, F), strides)

    def backward_cell(running, cell_id):
        grad_rbf, grad_filter = running
        brick, pos_x, pos_y, pos_z = locate(cell_id)
        window_geometry = cell_window(geometry_ext, brick, pos_x, pos_y, pos_z)
        gaussians, pre_filter, squashed, filters, weight = pair_tile(window_geometry, rbf_weight, filter_weight)
        sources = cell_window(hidden_ext, brick, pos_x, pos_y, pos_z).reshape(27 * P_SIZE, F)
        arriving = cell_window(cotangent_ext, brick, pos_x, pos_y, pos_z).reshape(27 * P_SIZE, F)
        own_cotangent = arriving.reshape(27, P_SIZE, F)[13]
        pair_grad = (own_cotangent.astype(jnp.float32)[:, None, :] * sources.astype(jnp.float32)[None, :, :] * weight.reshape(P_SIZE, 27 * P_SIZE)[:, :, None]).astype(jnp.bfloat16).reshape(P_SIZE * 27 * P_SIZE, F)
        grad_filter = grad_filter + lax.dot_general(squashed, pair_grad, (((0,), (0,)), ((), ())), preferred_element_type=jnp.float32)
        back_squash = lax.dot_general(pair_grad, filter_weight, (((1,), (1,)), ((), ())), preferred_element_type=jnp.float32)
        back_pre = (back_squash * jax.nn.sigmoid(pre_filter)).astype(jnp.bfloat16)
        grad_rbf = grad_rbf + jnp.dot(gaussians, back_pre, preferred_element_type=jnp.float32)
        back_hidden = window_geometry[13, 3, :][:, None] * jnp.einsum('jf,ijf->if', arriving.astype(jnp.float32), filters.reshape(P_SIZE, 27 * P_SIZE, F).astype(jnp.float32))
        return ((grad_rbf, grad_filter), back_hidden)
    starting = (jnp.zeros((K, F), jnp.float32), jnp.zeros((F, F), jnp.float32))
    (grad_rbf, grad_filter), back_hidden = lax.scan(backward_cell, starting, jnp.arange(NCELL, dtype=jnp.int32))
    back_low = back_hidden.reshape(NCELL * P_SIZE, F).astype(jnp.bfloat16)
    grad_in = jnp.dot(flat_features.T, back_low, preferred_element_type=jnp.float32)
    return (updated.reshape(NCELL, P_SIZE, F), (grad_in, grad_mid, grad_out, grad_rbf, grad_filter), energy_sum, live_total)

def reference(features, offsets, counts, in_weight, mid_weight, out_weight, rbf_weight, filter_weight, readout, target):
    outputs = []
    totals = (jnp.zeros((F, F), jnp.float32), jnp.zeros((F, F), jnp.float32), jnp.zeros((F, F), jnp.float32), jnp.zeros((K, F), jnp.float32), jnp.zeros((F, F), jnp.float32))
    for snapshot_id in range(SNAPS):
        updated, grads, energy_sum, live_total = snapshot(features[snapshot_id], offsets[snapshot_id], counts[snapshot_id], in_weight, mid_weight, out_weight, rbf_weight, filter_weight, readout)
        factor = 2.0 * (energy_sum / live_total - target[snapshot_id]) / live_total
        totals = tuple((totals[member] + factor * grads[member] for member in range(5)))
        outputs.append(updated)
    return (jnp.stack(outputs), totals[0], totals[1], totals[2], totals[3], totals[4])
```

```python
import math

import jax
import jax.numpy as jnp
from jax import lax
from jax.sharding import PartitionSpec as P

K = 25
BX = 2
BY = 4
BZ = 4
DEV_X = 1
DEV_Y = 2
DEV_Z = 4


cutoff = 1.0
block_cells = 8


def passed_along(value, axis, steps):
    count = lax.axis_size(axis)
    pairs = [(source, (source + steps) % count) for source in range(count)]
    return lax.ppermute(value, axis, pairs)


def shifted_ssp(values):
    return jax.nn.softplus(values) - math.log(2.0)


def pair_tile(window_geometry, rbf_weight, filter_weight):
    slot_count = window_geometry.shape[2]
    centre = jnp.arange(27)
    cell_shift = jnp.stack([centre // 9 - 1, centre // 3 % 3 - 1, centre % 3 - 1], axis=1).astype(
        jnp.float32
    )
    own_places = window_geometry[13, :3, :]
    neighbour_places = window_geometry[:, :3, :] + cell_shift[:, :, None]
    separation = neighbour_places[None, :, :, :] - jnp.transpose(own_places)[:, None, :, None]
    distance = jnp.sqrt(jnp.sum(separation * separation, axis=2))
    slots_here = jnp.arange(slot_count)
    itself = (centre[None, :, None] == 13) & (
        slots_here[None, None, :] == slots_here[:, None, None]
    )
    inside = (distance < cutoff) & jnp.logical_not(itself)
    smooth = 0.5 * (jnp.cos(math.pi * distance / cutoff) + 1.0)
    weight = jnp.where(inside, smooth, 0.0) * window_geometry[None, :, 3, :]
    distance = distance.reshape(-1)
    weight = weight.reshape(-1)
    centers = jnp.arange(K).astype(jnp.float32) * (cutoff / (K - 1))
    sharpness = (K - 1) * (K - 1) / 2.0
    gaussians = jnp.exp(-sharpness * (distance[None, :] - centers[:, None]) ** 2).astype(
        jnp.bfloat16
    )
    pre_filter = lax.dot_general(
        gaussians, rbf_weight, (((0,), (0,)), ((), ())), preferred_element_type=jnp.float32
    )
    squashed = shifted_ssp(pre_filter).astype(jnp.bfloat16)
    filter_base = jnp.dot(squashed, filter_weight, preferred_element_type=jnp.float32)
    filters = (filter_base * weight[:, None]).astype(jnp.bfloat16)
    return (gaussians, pre_filter, squashed, filters, weight)


def cell_window(extended, pos_x, pos_y, pos_z):
    corner = (pos_x, pos_y, pos_z) + (0,) * (extended.ndim - 3)
    shape_out = (3, 3, 3) + extended.shape[3:]
    return lax.dynamic_slice(extended, corner, shape_out).reshape((27,) + extended.shape[3:])


def extend_brick(brick, strides, sender):
    for axis_pos in range(3):
        extent = brick.shape[axis_pos]
        rims = []
        for direction in (1, -1):
            layer = extent - 1 if direction == 1 else 0
            rim_piece = lax.slice_in_dim(brick, layer, layer + 1, axis=axis_pos)
            rims.append(sender(rim_piece, direction * strides[axis_pos]))
        brick = jnp.concatenate([rims[0], brick, rims[1]], axis=axis_pos)
    return brick


def fold_back(accumulator, strides, sender):
    for axis_pos in (2, 1, 0):
        extent = accumulator.shape[axis_pos]
        inner_part = lax.slice_in_dim(accumulator, 1, extent - 1, axis=axis_pos)
        for direction in (1, -1):
            layer = extent - 1 if direction == 1 else 0
            target_layer = 0 if direction == 1 else extent - 3
            rim_piece = lax.slice_in_dim(accumulator, layer, layer + 1, axis=axis_pos)
            received = sender(rim_piece, direction * strides[axis_pos])
            current = lax.slice_in_dim(inner_part, target_layer, target_layer + 1, axis=axis_pos)
            inner_part = lax.dynamic_update_slice_in_dim(
                inner_part, current + received, target_layer, axis=axis_pos
            )
        accumulator = inner_part
    return accumulator


def split_parts(value):
    high = lax.reduce_precision(value, 8, 7)
    middle = lax.reduce_precision(value - high, 8, 7)
    low = lax.reduce_precision(value - high - middle, 8, 7)
    return [high, middle, low]


def reduced_gradients(rows, grad_rbf, energy_sum, live_total, target):
    both = ("space", "dp")
    space_count = lax.axis_size("space")
    snaps = lax.axis_size("dp")
    devices = space_count * snaps
    width = rows.shape[1]
    extra = jnp.pad(grad_rbf.reshape(-1, 8), ((0, devices - K * width // 8), (0, 0)))
    facts = jnp.stack(split_parts(energy_sum) + split_parts(target) + [live_total])
    facts = jnp.broadcast_to(jnp.pad(facts, (0, width - 15))[None, :], (devices, width - 8))
    second = jnp.concatenate([extra, facts], axis=1)
    sent = jnp.stack([rows, second], axis=1).astype(jnp.bfloat16)
    got = lax.all_to_all(sent, both, 0, 0, tiled=True).astype(jnp.float32)
    per_snapshot = jnp.sum(got.reshape(space_count, snaps, 2, width), axis=0)
    energy = jnp.sum(per_snapshot[:, 1, 8:11], axis=1)
    live = per_snapshot[:, 1, 14]
    targets = jnp.sum(got.reshape(space_count, snaps, 2, width)[0, :, 1, 11:14], axis=1)
    factor = 2.0 * (energy / live - targets) / live
    finished = jnp.sum(per_snapshot * factor[:, None, None], axis=0).astype(jnp.bfloat16)
    back = lax.all_to_all(
        jnp.broadcast_to(finished[None], (devices, 2, width)), both, 0, 0, tiled=True
    ).astype(jnp.float32)
    full = back[:, 0, :].reshape(4, width, width)
    rbf = back[: K * width // 8, 1, :8].reshape(K, width)
    return full[0], full[1], full[2], rbf, full[3]


def shards(
    features,
    offsets,
    counts,
    in_weight,
    mid_weight,
    out_weight,
    rbf_weight,
    filter_weight,
    readout,
    target,
):
    strides = (DEV_X, DEV_Y, DEV_Z)
    cell_count = features.shape[1]
    slot_count = features.shape[2]
    feature_width = features.shape[3]
    occupied = (jnp.arange(slot_count)[None, :] < counts[0][:, None]).astype(jnp.float32)
    geometry = jnp.concatenate([offsets[0], occupied[:, None, :]], axis=1).reshape(
        BX, BY, BZ, 4, slot_count
    )

    def geometry_send(rim_piece, moved_by):
        return passed_along(rim_piece, "space", moved_by)

    def feature_send(rim_piece, moved_by):
        return passed_along(rim_piece, "space", moved_by)

    def sums_send(rim_piece, moved_by):
        return passed_along(rim_piece, "space", moved_by)

    geometry_ext = extend_brick(geometry, strides, geometry_send)
    flat_features = features[0].reshape(cell_count * slot_count, feature_width)
    hidden = jnp.dot(flat_features, in_weight, preferred_element_type=jnp.float32).astype(
        jnp.bfloat16
    )
    widened = extend_brick(
        hidden.reshape(BX, BY, BZ, slot_count, feature_width), strides, feature_send
    )
    step_total = cell_count // block_cells
    block_offsets = jnp.arange(block_cells)

    def locate(step_index):
        cell_ids = step_index * block_cells + block_offsets
        return (cell_ids // (BY * BZ), cell_ids // BZ % BY, cell_ids % BZ)

    def forward_cell(pos_x, pos_y, pos_z):
        window_geometry = cell_window(geometry_ext, pos_x, pos_y, pos_z)
        pieces = pair_tile(window_geometry, rbf_weight, filter_weight)
        filters = pieces[3].reshape(slot_count, 27 * slot_count, feature_width)
        sources = cell_window(widened, pos_x, pos_y, pos_z).reshape(27 * slot_count, feature_width)
        return jnp.einsum("jf,ijf->if", sources, filters, preferred_element_type=jnp.float32)

    def forward_step(step_index):
        pos_x, pos_y, pos_z = locate(step_index)
        return jax.vmap(forward_cell, in_axes=(0, 0, 0))(pos_x, pos_y, pos_z)

    message = lax.map(forward_step, jnp.arange(step_total)).reshape(
        cell_count * slot_count, feature_width
    )
    message_low = message.astype(jnp.bfloat16)
    inner = jnp.dot(message_low, mid_weight, preferred_element_type=jnp.float32)
    activation = shifted_ssp(inner).astype(jnp.bfloat16)
    updated = (
        flat_features.astype(jnp.float32)
        + jnp.dot(activation, out_weight, preferred_element_type=jnp.float32)
    ).astype(jnp.bfloat16)
    occupied_flat = occupied.reshape(-1)
    energy = jnp.dot(updated, readout, preferred_element_type=jnp.float32)
    energy_sum = jnp.sum(energy * occupied_flat)
    live_total = jnp.sum(occupied_flat)
    contract_rows = (((0,), (0,)), ((), ()))
    start_grad = (occupied_flat[:, None] * readout[None, :].astype(jnp.float32)).astype(
        jnp.bfloat16
    )
    grad_out = lax.dot_general(
        activation, start_grad, contract_rows, preferred_element_type=jnp.float32
    )
    back_act = lax.dot_general(
        start_grad, out_weight, (((1,), (1,)), ((), ())), preferred_element_type=jnp.float32
    )
    back_inner = (back_act * jax.nn.sigmoid(inner)).astype(jnp.bfloat16)
    grad_mid = lax.dot_general(
        message_low, back_inner, contract_rows, preferred_element_type=jnp.float32
    )
    cotangent = lax.dot_general(
        back_inner, mid_weight, (((1,), (1,)), ((), ())), preferred_element_type=jnp.float32
    ).astype(jnp.bfloat16)
    cotangent_brick = cotangent.reshape(BX, BY, BZ, slot_count, feature_width)

    def pair_backward(pos_x, pos_y, pos_z):
        window_geometry = cell_window(geometry_ext, pos_x, pos_y, pos_z)
        gaussians, pre_filter, squashed, filters, weight = pair_tile(
            window_geometry, rbf_weight, filter_weight
        )
        sources = cell_window(widened, pos_x, pos_y, pos_z).reshape(27 * slot_count, feature_width)
        own_cotangent = lax.dynamic_slice(
            cotangent_brick, (pos_x, pos_y, pos_z, 0, 0), (1, 1, 1, slot_count, feature_width)
        ).reshape(slot_count, feature_width)
        pair_grad = (
            (
                own_cotangent.astype(jnp.float32)[:, None, :]
                * sources.astype(jnp.float32)[None, :, :]
                * weight.reshape(slot_count, 27 * slot_count)[:, :, None]
            )
            .astype(jnp.bfloat16)
            .reshape(-1, feature_width)
        )
        filter_part = lax.dot_general(
            squashed, pair_grad, contract_rows, preferred_element_type=jnp.float32
        )
        back_squash = lax.dot_general(
            pair_grad, filter_weight, (((1,), (1,)), ((), ())), preferred_element_type=jnp.float32
        )
        back_pre = (back_squash * jax.nn.sigmoid(pre_filter)).astype(jnp.bfloat16)
        rbf_part = jnp.dot(gaussians, back_pre, preferred_element_type=jnp.float32)
        return (
            rbf_part,
            filter_part,
            filters.reshape(slot_count, 27 * slot_count, feature_width),
            own_cotangent,
            window_geometry[13, 3, :],
        )

    batched = jax.vmap(pair_backward, in_axes=(0, 0, 0))
    grad_start = (
        jnp.zeros((K, feature_width), jnp.float32),
        jnp.zeros((feature_width, feature_width), jnp.float32),
    )
    accumulator = jnp.zeros((BX + 2, BY + 2, BZ + 2, slot_count, feature_width), jnp.float32)

    def send_step(running, step_index):
        grad_rbf_now, grad_filter_now, gathered_sums = running
        pos_x, pos_y, pos_z = locate(step_index)
        rbf_part, filter_part, filters, own_cotangent, own_live = batched(pos_x, pos_y, pos_z)
        spread = jnp.einsum(
            "cif,cijf->cjf", own_cotangent, filters, preferred_element_type=jnp.float32
        )
        for member in range(block_cells):
            corner = (pos_x[member], pos_y[member], pos_z[member], 0, 0)
            current = lax.dynamic_slice(gathered_sums, corner, (3, 3, 3, slot_count, feature_width))
            gathered_sums = lax.dynamic_update_slice(
                gathered_sums,
                current + spread[member].reshape(3, 3, 3, slot_count, feature_width),
                corner,
            )
        return (
            (
                grad_rbf_now + jnp.sum(rbf_part, axis=0),
                grad_filter_now + jnp.sum(filter_part, axis=0),
                gathered_sums,
            ),
            None,
        )

    (grad_rbf, grad_filter, accumulator), unused = lax.scan(
        send_step, (grad_start[0], grad_start[1], accumulator), jnp.arange(step_total)
    )
    back_hidden = fold_back(accumulator, strides, sums_send)
    back_low = back_hidden.reshape(cell_count * slot_count, feature_width).astype(jnp.bfloat16)
    grad_in = lax.dot_general(
        flat_features, back_low, contract_rows, preferred_element_type=jnp.float32
    )
    rows = jnp.concatenate([grad_in, grad_mid, grad_out, grad_filter], axis=0)
    totals = reduced_gradients(rows, grad_rbf, energy_sum, live_total, target[0])
    return (
        updated.reshape(1, cell_count, slot_count, feature_width),
        totals[0],
        totals[1],
        totals[2],
        totals[3],
        totals[4],
    )


def solution(mesh):
    placed = (
        P("dp", "space", None, None),
        P("dp", "space", None, None),
        P("dp", "space"),
        P(),
        P(),
        P(),
        P(),
        P(),
        P(),
        P("dp"),
    )
    return jax.shard_map(
        shards,
        mesh=mesh,
        in_specs=placed,
        out_specs=(P("dp", "space", None, None), P(), P(), P(), P(), P()),
        check_vma=False,
    )
```

```python
import math

import jax
import jax.numpy as jnp
from jax import lax
from jax.experimental import pallas as pl
from jax.experimental.pallas import tpu as pltpu
from jax.sharding import PartitionSpec as P

K = 25
BX = 2
BY = 4
BZ = 4
DEV_X = 1
DEV_Y = 2
DEV_Z = 4


CELLS = 32
LANES = 128
PAIRS = 112
cutoff = 1.0


def passed_along(value, axis, steps):
    count = lax.axis_size(axis)
    pairs = [(source, (source + steps) % count) for source in range(count)]
    return lax.ppermute(value, axis, pairs)


def extend_brick(brick, strides, sender):
    for axis_pos in range(3):
        extent = brick.shape[axis_pos]
        rims = []
        for direction in (1, -1):
            layer = extent - 1 if direction == 1 else 0
            rim_piece = lax.slice_in_dim(brick, layer, layer + 1, axis=axis_pos)
            rims.append(sender(rim_piece, direction * strides[axis_pos]))
        brick = jnp.concatenate([rims[0], brick, rims[1]], axis=axis_pos)
    return brick


def column_of(values, mask):
    return jnp.sum(jnp.where(mask, values, 0.0), axis=1, keepdims=True)


def dot_rows(left, right):
    return lax.dot_general(
        left, right, (((0,), (0,)), ((), ())), preferred_element_type=jnp.float32
    )


def dot_last(left, right):
    return lax.dot_general(
        left, right, (((1,), (1,)), ((), ())), preferred_element_type=jnp.float32
    )


def softplus_half(values):
    return jnp.maximum(values, 0.0) + jnp.log(1.0 + jnp.exp(-jnp.abs(values))) - math.log(2.0)


def logistic(values):
    return 0.5 * jnp.tanh(0.5 * values) + 0.5


def brick_kernel(
    wide_ref,
    own_ref,
    geo_ref,
    in_ref,
    mid_ref,
    out_ref,
    rbf_ref,
    filter_ref,
    readout_ref,
    updated_ref,
    rows_ref,
    grad_rbf_ref,
    energy_ref,
    hidden_ext,
    feature_ext,
    hidden_win,
    feature_win,
    gathered,
    expanded,
    distance_ref,
    omega_ref,
    gauss_ref,
    squashed_ref,
    slope_ref,
    filters_ref,
    product_ref,
    message_ref,
    cotangent_ref,
    grad_ref,
    pre_ref,
    spread_ref,
):
    f32 = jnp.float32
    bf16 = jnp.bfloat16
    feature_ext[...] = wide_ref[...].astype(f32)
    hidden_ext[...] = (
        jnp.dot(wide_ref[...], in_ref[...], preferred_element_type=f32).astype(bf16).astype(f32)
    )
    pad = jnp.zeros((LANES - 108, LANES), f32)
    for cell in range(CELLS):
        pos_x, pos_y, pos_z = cell // 16, cell // 4 % 4, cell % 4
        for member in range(9):
            start = ((pos_x + member // 3) * 6 + pos_y + member % 3) * 24 + 4 * pos_z
            place = cell * LANES + 12 * member
            hidden_win[place : place + 12, :] = hidden_ext[start : start + 12, :]
            feature_win[place : place + 12, :] = feature_ext[start : start + 12, :]
        hidden_win[cell * LANES + 108 : (cell + 1) * LANES, :] = pad
        feature_win[cell * LANES + 108 : (cell + 1) * LANES, :] = pad

    total = jnp.zeros((32, 4 * LANES), f32)
    source = lax.broadcasted_iota(jnp.int32, (24, 4 * LANES), 0)
    column = lax.broadcasted_iota(jnp.int32, (24, 4 * LANES), 1)
    lane_of = column % LANES
    for member in range(9):
        pos_x, pos_y = member // 3, member % 3
        local = lane_of - 12 * member
        chosen = (local >= 0) & (local < 12) & (source == 4 * (column // LANES) + local)
        picked = jnp.concatenate(
            [
                geo_ref[pos_x * 24 + pos_y * 4 : pos_x * 24 + pos_y * 4 + 16, :],
                geo_ref[(pos_x + 1) * 24 + pos_y * 4 : (pos_x + 1) * 24 + pos_y * 4 + 16, :],
            ],
            axis=0,
        )
        total = total + jnp.dot(
            picked,
            jnp.where(chosen, 1.0, 0.0).astype(f32),
            preferred_element_type=f32,
            precision=lax.Precision.HIGHEST,
        )
    gathered[...] = total
    for cell in range(CELLS):
        for part in range(4):
            row = (cell // 4) * 4 + part
            here = cell % 4 * LANES
            expanded[part, 4 * cell : 4 * cell + 4, :] = jnp.broadcast_to(
                gathered[row : row + 1, here : here + LANES], (4, LANES)
            )
    lane = lax.broadcasted_iota(jnp.int32, (LANES, LANES), 1)
    slot = lax.broadcasted_iota(jnp.int32, (LANES, LANES), 0) % 4
    itself = lane == 52 + slot
    member = lane // 12
    shifts = (member // 3 - 1, member % 3 - 1, lane % 12 // 4 - 1)
    squares = jnp.zeros((LANES, LANES), f32)
    for part in range(3):
        places = expanded[part]
        own = column_of(places, itself)
        separation = places + shifts[part].astype(f32) - own
        squares = squares + separation * separation
    distance = jnp.sqrt(squares)
    occupied = expanded[3]
    live = column_of(occupied, itself)
    inside = (distance < cutoff) & jnp.logical_not(itself) & (lane < 108)
    smooth = 0.5 * (jnp.cos(math.pi * distance / cutoff) + 1.0)
    omega = jnp.where(inside, smooth, 0.0) * occupied
    distance_ref[...] = distance
    omega_ref[...] = omega

    order = lax.broadcasted_iota(jnp.int32, (32, LANES), 0)
    centers = order.astype(f32) * (cutoff / (K - 1))
    sharpness = (K - 1) * (K - 1) / 2.0
    empty = jnp.zeros((LANES - PAIRS, LANES), bf16)

    def forward(cell, carry):
        tiles = []
        for slot_id in range(4):
            at = pl.ds(4 * cell + slot_id, 1)
            away = distance_ref[at, :] - centers
            tile = jnp.exp(-sharpness * away * away)
            weight = omega_ref[at, :]
            high = weight.astype(bf16).astype(f32)
            middle = (weight - high).astype(bf16).astype(f32)
            low = weight - high - middle
            extra = jnp.where(order == K, high, jnp.where(order == K + 1, middle, low))
            tiles.append(
                jnp.where(order < K, tile, jnp.where(order < K + 3, extra, 0.0)).astype(bf16)
            )
        gauss = jnp.concatenate(tiles, axis=1)
        gauss_ref[cell] = gauss
        both = dot_rows(gauss, rbf_ref[...])
        base_row = pl.multiple_of(cell * LANES, LANES)
        hidden = hidden_win[pl.ds(base_row, PAIRS), :]
        for slot_id in range(4):
            first = slot_id * LANES
            pre = both[first : first + PAIRS, :LANES]
            squashed = jnp.log(1.0 + jnp.exp(pre)) - math.log(2.0)
            squashed_ref[cell, first : first + PAIRS, :] = squashed.astype(bf16)
            squashed_ref[cell, first + PAIRS : first + LANES, :] = empty
            slope_ref[cell, first : first + PAIRS, :] = logistic(pre)
        base = jnp.dot(squashed_ref[cell], filter_ref[...], preferred_element_type=f32)
        for slot_id in range(4):
            first = slot_id * LANES
            weight = both[first : first + PAIRS, LANES:]
            filters = (base[first : first + PAIRS, :] * weight).astype(bf16)
            filters_ref[cell, first : first + PAIRS, :] = filters
            product_ref[cell, first : first + PAIRS, :] = hidden * weight
            message_ref[pl.ds(4 * cell + slot_id, 1), :] = jnp.sum(
                hidden * filters.astype(f32), axis=0, keepdims=True
            )
        return carry

    lax.fori_loop(0, CELLS, forward, 0)

    message = message_ref[...].astype(bf16)
    inner = jnp.dot(message, mid_ref[...], preferred_element_type=f32)
    activation = softplus_half(inner).astype(bf16)
    updated = (
        own_ref[...].astype(f32) + jnp.dot(activation, out_ref[...], preferred_element_type=f32)
    ).astype(bf16)
    updated_ref[...] = updated
    readout = readout_ref[...].astype(f32)
    start_grad = (live * readout).astype(bf16)
    energy = jnp.sum(updated.astype(f32) * readout * live, axis=0, keepdims=True)
    energy_ref[...] = jnp.broadcast_to(energy, (8, LANES))
    rows_ref[2 * LANES : 3 * LANES, :] = dot_rows(activation, start_grad)
    back_inner = (dot_last(start_grad, out_ref[...]) * logistic(inner)).astype(bf16)
    rows_ref[LANES : 2 * LANES, :] = dot_rows(message, back_inner)
    cotangent_ref[...] = dot_last(back_inner, mid_ref[...]).astype(bf16).astype(f32)
    rows_ref[0:LANES, :] = jnp.zeros((LANES, LANES), f32)
    rows_ref[3 * LANES : 4 * LANES, :] = jnp.zeros((LANES, LANES), f32)
    grad_rbf_ref[...] = jnp.zeros((32, LANES), f32)
    spread_ref[...] = jnp.zeros((LANES, LANES), bf16)
    grad_ref[...] = jnp.zeros((4 * LANES, LANES), bf16)
    pre_ref[...] = jnp.zeros((4 * LANES, LANES), bf16)

    def backward(cell, carry):
        spread = jnp.zeros((PAIRS, LANES), f32)
        for slot_id in range(4):
            first = slot_id * LANES
            cotangent = cotangent_ref[pl.ds(4 * cell + slot_id, 1), :]
            grad_ref[first : first + PAIRS, :] = (
                cotangent * product_ref[cell, first : first + PAIRS, :]
            ).astype(bf16)
            spread = spread + cotangent * filters_ref[cell, first : first + PAIRS, :].astype(f32)
        spread_ref[0:PAIRS, :] = spread.astype(bf16)
        back = dot_last(grad_ref[...], filter_ref[...])
        for slot_id in range(4):
            first = slot_id * LANES
            pre_ref[first : first + PAIRS, :] = (
                back[first : first + PAIRS, :] * slope_ref[cell, first : first + PAIRS, :]
            ).astype(bf16)
        rows_ref[3 * LANES : 4 * LANES, :] += dot_rows(squashed_ref[cell], grad_ref[...])
        grad_rbf_ref[...] += jnp.dot(gauss_ref[cell], pre_ref[...], preferred_element_type=f32)
        base_row = pl.multiple_of(cell * LANES, LANES)
        rows_ref[0:LANES, :] += dot_rows(
            feature_win[pl.ds(base_row, LANES), :].astype(bf16), spread_ref[...]
        )
        return carry

    lax.fori_loop(0, CELLS, backward, 0)


def brick_pass(wide, own, geometry, in_weight, mid_weight, out_weight, rbf_weight, filter_weight, readout, interpret=False):
    f32 = jnp.float32
    bf16 = jnp.bfloat16
    left = jnp.pad(rbf_weight, ((0, 32 - K), (0, LANES)))
    ones = jnp.pad(jnp.ones((3, LANES), bf16), ((K, 32 - K - 3), (LANES, 0)))
    tall = CELLS * LANES
    return pl.pallas_call(
        brick_kernel,
        out_shape=(
            jax.ShapeDtypeStruct((LANES, LANES), bf16),
            jax.ShapeDtypeStruct((4 * LANES, LANES), f32),
            jax.ShapeDtypeStruct((32, LANES), f32),
            jax.ShapeDtypeStruct((8, LANES), f32),
        ),
        in_specs=[pl.BlockSpec(memory_space=pltpu.VMEM)] * 9,
        out_specs=[pl.BlockSpec(memory_space=pltpu.VMEM)] * 4,
        scratch_shapes=[
            pltpu.VMEM((576, LANES), f32),
            pltpu.VMEM((576, LANES), f32),
            pltpu.VMEM((tall, LANES), f32),
            pltpu.VMEM((tall, LANES), f32),
            pltpu.VMEM((32, 4 * LANES), f32),
            pltpu.VMEM((4, LANES, LANES), f32),
            pltpu.VMEM((LANES, LANES), f32),
            pltpu.VMEM((LANES, LANES), f32),
            pltpu.VMEM((CELLS, 32, 4 * LANES), bf16),
            pltpu.VMEM((CELLS, 4 * LANES, LANES), bf16),
            pltpu.VMEM((CELLS, 4 * LANES, LANES), f32),
            pltpu.VMEM((CELLS, 4 * LANES, LANES), bf16),
            pltpu.VMEM((CELLS, 4 * LANES, LANES), f32),
            pltpu.VMEM((LANES, LANES), f32),
            pltpu.VMEM((LANES, LANES), f32),
            pltpu.VMEM((4 * LANES, LANES), bf16),
            pltpu.VMEM((4 * LANES, LANES), bf16),
            pltpu.VMEM((LANES, LANES), bf16),
        ],
        compiler_params=pltpu.CompilerParams(vmem_limit_bytes=50 * 1024 * 1024),
        interpret=interpret,
    )(
        wide,
        own,
        geometry,
        in_weight,
        mid_weight,
        out_weight,
        left + ones,
        filter_weight,
        readout.reshape(1, LANES),
    )


def split_parts(value):
    high = lax.reduce_precision(value, 8, 7)
    middle = lax.reduce_precision(value - high, 8, 7)
    low = lax.reduce_precision(value - high - middle, 8, 7)
    return [high, middle, low]


def reduced_gradients(rows, grad_rbf, energy_sum, live_total, target):
    both = ("space", "dp")
    space_count = lax.axis_size("space")
    snaps = lax.axis_size("dp")
    devices = space_count * snaps
    width = rows.shape[1]
    extra = jnp.pad(grad_rbf.reshape(-1, 8), ((0, devices - K * width // 8), (0, 0)))
    facts = jnp.stack(split_parts(energy_sum) + split_parts(target) + [live_total])
    facts = jnp.broadcast_to(jnp.pad(facts, (0, width - 15))[None, :], (devices, width - 8))
    second = jnp.concatenate([extra, facts], axis=1)
    sent = jnp.stack([rows, second], axis=1).astype(jnp.bfloat16)
    got = lax.all_to_all(sent, both, 0, 0, tiled=True).astype(jnp.float32)
    per_snapshot = jnp.sum(got.reshape(space_count, snaps, 2, width), axis=0)
    energy = jnp.sum(per_snapshot[:, 1, 8:11], axis=1)
    live = per_snapshot[:, 1, 14]
    targets = jnp.sum(got.reshape(space_count, snaps, 2, width)[0, :, 1, 11:14], axis=1)
    factor = 2.0 * (energy / live - targets) / live
    finished = jnp.sum(per_snapshot * factor[:, None, None], axis=0).astype(jnp.bfloat16)
    back = lax.all_to_all(
        jnp.broadcast_to(finished[None], (devices, 2, width)), both, 0, 0, tiled=True
    ).astype(jnp.float32)
    full = back[:, 0, :].reshape(4, width, width)
    rbf = back[: K * width // 8, 1, :8].reshape(K, width)
    return full[0], full[1], full[2], rbf, full[3]


def shards(
    features,
    offsets,
    counts,
    in_weight,
    mid_weight,
    out_weight,
    rbf_weight,
    filter_weight,
    readout,
    target,
):
    strides = (DEV_X, DEV_Y, DEV_Z)
    cell_count = features.shape[1]
    slot_count = features.shape[2]
    feature_width = features.shape[3]
    occupied = (jnp.arange(slot_count)[None, :] < counts[0][:, None]).astype(jnp.float32)
    geometry = jnp.concatenate([offsets[0], occupied[:, None, :]], axis=1).reshape(
        BX, BY, BZ, 4, slot_count
    )

    def geometry_send(rim_piece, moved_by):
        return passed_along(rim_piece, "space", moved_by)

    def feature_send(rim_piece, moved_by):
        return passed_along(rim_piece, "space", moved_by)

    geometry_ext = extend_brick(geometry, strides, geometry_send)
    widened = extend_brick(
        features[0].reshape(BX, BY, BZ, slot_count, feature_width), strides, feature_send
    )
    live_total = jnp.sum(occupied)
    updated, rows, grad_rbf, energy = brick_pass(
        widened.reshape(-1, feature_width),
        features[0].reshape(cell_count * slot_count, feature_width),
        jnp.transpose(geometry_ext, (0, 1, 3, 2, 4)).reshape(96, 24),
        in_weight,
        mid_weight,
        out_weight,
        rbf_weight,
        filter_weight,
        readout,
    )
    energy_sum = jnp.sum(energy[0])
    grad_rbf = grad_rbf[:K]
    totals = reduced_gradients(rows, grad_rbf, energy_sum, live_total, target[0])
    return (
        updated.reshape(1, cell_count, slot_count, feature_width),
        totals[0],
        totals[1],
        totals[2],
        totals[3],
        totals[4],
    )


def solution(mesh):
    placed = (
        P("dp", "space", None, None),
        P("dp", "space", None, None),
        P("dp", "space"),
        P(),
        P(),
        P(),
        P(),
        P(),
        P(),
        P("dp"),
    )
    return jax.shard_map(
        shards,
        mesh=mesh,
        in_specs=placed,
        out_specs=(P("dp", "space", None, None), P(), P(), P(), P(), P()),
        check_vma=False,
    )
```
